32 devices in a mesh: seq: 8 (over z, x), tp: 4 (over y, core).
Axes of the slice: x: 2, y: 2, z: 4, core: 2. Of those that a mesh axis runs over, the one named last changes fastest.
Arguments:
- tokens: bfloat16 [4096, 4096], P(('seq', 'tp')), may hold values from -64 to 64, as said below
- joined_projection_weight: bfloat16 [4096, 6144], P(None, 'tp'), may hold values from -0.09375 to 0.09375
- adapter_down_weight: bfloat16 [4096, 64], replicated, may hold values from -0.09375 to 0.09375
- adapter_up_weight: bfloat16 [64, 6144], P(None, 'tp'), may hold values from -0.75 to 0.75
- document_index: int32 [4096], replicated, may hold values from 0 to 3, as said below
- query_to_key_head: int32 [32], replicated, may hold values from 0 to 7, as said below
Outputs:
- context: bfloat16 [4096, 4096], P(('seq', 'tp'))
The draws below stay inside these ranges and needn't reach their ends.
Inputs may be any that keep to these rules, and one draw needn't show every extreme that they name: `tokens`: rows of order one, except in the hidden draw where some rows have larger scales. `query_to_key_head`: each of 0 to 7 is named by exactly 4 query heads. `document_index`: never falling, starting at 0; each of the 4 documents covers 4096 / 16 or more positions.
All inputs are finite; a program needn't handle non-finite values.
Results may differ from the reference program's by a relative error of at most 0.012.
The reference program's roundings to bfloat16 on the way count: a program that leaves them out, or rounds other values in their place, can miss the bound.
Values may be sent and summed in bfloat16 or wider, within the bound.
A program may use at most 128 MiB of HBM per device.

```python
import jax
import jax.numpy as jnp
from jax import lax

MODEL_WIDTH = 4096
H = 32
KV = 8
DH = 128
ADAPTER_RANK = 64
DOCS = 4
S = 4096
JOINED_COLUMNS = 6144
N_TP = 4


def draw_tokens(key, part):
    noise_key = jax.random.fold_in(key, 0)
    drawn = jax.random.normal(noise_key, (S, MODEL_WIDTH), jnp.float32)
    return jnp.clip(drawn, -64.0, 64.0).astype(jnp.bfloat16)


def draw_document_index(key, part):
    length_key = jax.random.fold_in(key, 7)
    lengths = jax.random.randint(length_key, (DOCS - 1,), S // 16, 5 * S // 16, dtype=jnp.int32)
    bounds = jnp.cumsum(lengths).astype(jnp.int32)
    places = jnp.arange(S, dtype=jnp.int32)
    return jnp.sum((places[:, None] >= bounds[None, :]).astype(jnp.int32), axis=1).astype(jnp.int32)


def draw_query_to_key_head(key, part):
    order = jax.random.permutation(key, H)
    return (order % KV).astype(jnp.int32)


def level_of(rng, extent, shards, least, largest):
    level, own = 1.0, jax.random.fold_in(rng, 6)
    for dim, blocks in shards:
        heights = jnp.exp(jax.random.uniform(jax.random.fold_in(own, dim), (blocks,), jnp.float32, least / len(shards), largest / len(shards)))
        level = level * jnp.repeat(heights, extent[dim] // blocks).reshape([-1 if axis == dim else 1 for axis in range(len(extent))])
    return level


def gaussian(key, dims, spread, limit, shards=(), kind=jnp.bfloat16):
    gain = level_of(key, dims, shards, -0.22, 0.18) if shards else 1.0
    result = jax.random.normal(key, dims, jnp.float32) * spread * gain
    return jnp.minimum(jnp.maximum(result, -limit), limit).astype(kind)


def setup_inputs(seed: int = 0) -> dict:
    splits = jax.random.split(jax.random.key(seed), 7)
    return {
        "tokens": draw_tokens(jax.random.fold_in(splits[6], 71), 0),
        "joined_projection_weight": gaussian(splits[1], (MODEL_WIDTH, JOINED_COLUMNS), MODEL_WIDTH ** -0.5, 0.09375, ((1, 4),)),
        "adapter_down_weight": gaussian(splits[2], (MODEL_WIDTH, ADAPTER_RANK), MODEL_WIDTH ** -0.5, 0.09375),
        "adapter_up_weight": gaussian(splits[3], (ADAPTER_RANK, JOINED_COLUMNS), ADAPTER_RANK ** -0.5, 0.75, ((1, 4),)),
        "document_index": draw_document_index(jax.random.fold_in(splits[6], 71), 0),
        "query_to_key_head": draw_query_to_key_head(jax.random.fold_in(splits[6], 71), 0),
    }


ADAPTER_SCALE = 0.5
THETA = 500000.0


def rotate(values, places):
    half_dim = values.shape[-1] // 2
    frequency = THETA ** (-(jnp.arange(half_dim, dtype=jnp.float32) * 2.0) / values.shape[-1])
    angles = places[:, None] * frequency[None, :]
    cosine = jnp.cos(angles)[:, None, :]
    sine_part = jnp.sin(angles)[:, None, :]
    front_half = values[..., :half_dim]
    back_half = values[..., half_dim:]
    return jnp.concatenate([front_half * cosine - back_half * sine_part, back_half * cosine + front_half * sine_part], axis=-1)


def reference(tokens, joined_projection_weight, adapter_down_weight, adapter_up_weight, document_index, query_to_key_head):
    projected_rows = jnp.dot(tokens, joined_projection_weight, preferred_element_type=jnp.float32)
    adapter_middle = jnp.dot(tokens, adapter_down_weight, preferred_element_type=jnp.float32).astype(jnp.bfloat16)
    joined_output = projected_rows + ADAPTER_SCALE * jnp.dot(adapter_middle, adapter_up_weight, preferred_element_type=jnp.float32)
    query_group = H // N_TP
    key_group = KV // N_TP
    grouped = joined_output.reshape(S, N_TP, (query_group + 2 * key_group) * DH)
    queries = grouped[:, :, :query_group * DH].reshape(S, H, DH)
    keys = grouped[:, :, query_group * DH:(query_group + key_group) * DH].reshape(S, KV, DH)
    values = grouped[:, :, (query_group + key_group) * DH:].reshape(S, KV, DH)
    places = jnp.arange(S, dtype=jnp.int32).astype(jnp.float32)
    q_rot = rotate(queries, places).astype(jnp.bfloat16)
    k_rot = rotate(keys, places).astype(jnp.bfloat16)
    v_half = values.astype(jnp.bfloat16)
    k_head = k_rot[:, query_to_key_head]
    v_head = v_half[:, query_to_key_head]
    scale = DH ** -0.5
    query_block = min(1024, S)
    key_places = jnp.arange(S, dtype=jnp.int32)

    def head_out(head_index):
        q_one = lax.dynamic_index_in_dim(q_rot, head_index, 1, keepdims=False)
        k_one = lax.dynamic_index_in_dim(k_head, head_index, 1, keepdims=False)
        v_one = lax.dynamic_index_in_dim(v_head, head_index, 1, keepdims=False)

        def block_out(block_index):
            start = (block_index * query_block).astype(jnp.int32)
            q_tile = lax.dynamic_slice_in_dim(q_one, start, query_block, 0)
            tile_places = start + jnp.arange(query_block, dtype=jnp.int32)
            tile_segments = lax.dynamic_slice_in_dim(document_index, start, query_block, 0)
            scores = jnp.dot(q_tile, k_one.T, preferred_element_type=jnp.float32) * scale
            allowed = (key_places[None, :] <= tile_places[:, None]) & (document_index[None, :] == tile_segments[:, None])
            scores = jnp.where(allowed, scores, -jnp.inf)
            row_max = jnp.max(scores, axis=-1, keepdims=True)
            powers = jnp.exp(scores - row_max)
            weights = powers.astype(jnp.bfloat16)
            numer = jnp.dot(weights, v_one, preferred_element_type=jnp.float32)
            return (numer / jnp.sum(powers, axis=-1, keepdims=True)).astype(jnp.bfloat16)

        return lax.map(block_out, jnp.arange(S // query_block, dtype=jnp.int32)).reshape(S, DH)

    per_head = lax.map(head_out, jnp.arange(H, dtype=jnp.int32))
    return jnp.transpose(per_head, (1, 0, 2)).reshape(S, H * DH)
```

```python
import functools

import jax
import jax.numpy as jnp
from jax import lax
from jax.experimental import pallas as pl
from jax.experimental.pallas import tpu as pltpu
from jax.sharding import PartitionSpec as P

H = 32
KV = 8
DH = 128
GROUP = H // KV

ADAPTER_SCALE = 0.5
THETA = 500000.0
NEG_BIG = -1e30
LOG2_E = 1.4426950408889634


def rope_tables(places):
    half = DH // 2
    frequency = THETA ** (-(jnp.arange(half, dtype=jnp.float32) * 2.0) / DH)
    angles = places[:, None] * frequency[None, :]
    cosine, sine = jnp.cos(angles), jnp.sin(angles)
    return jnp.concatenate([cosine, cosine], 1), jnp.concatenate([-sine, sine], 1)


def project_kernel(rotated_pairs, x_ref, w_ref, down_ref, up_ref, cos_ref, sin_ref, out_ref, mid_ref):
    step = pl.program_id(0)
    chunks, pair, rows, _ = out_ref.shape

    @pl.when(step == 0)
    def _():
        mid_ref[...] = jnp.dot(
            x_ref[...], down_ref[...], preferred_element_type=jnp.float32
        ).astype(jnp.bfloat16)

    joined = jnp.dot(x_ref[...], w_ref[...], preferred_element_type=jnp.float32)
    joined = joined + ADAPTER_SCALE * jnp.dot(
        mid_ref[...], up_ref[...], preferred_element_type=jnp.float32
    )

    def store(head, value):
        value = value.astype(jnp.bfloat16)
        for chunk in range(chunks):
            out_ref[chunk, head] = value[chunk * rows : (chunk + 1) * rows]

    @pl.when(step < rotated_pairs)
    def _():
        for head in range(pair):
            part = joined[:, head * DH : (head + 1) * DH]
            store(head, part * cos_ref[...] + pltpu.roll(part, DH // 2, 1) * sin_ref[...])

    @pl.when(step >= rotated_pairs)
    def _():
        for head in range(pair):
            store(head, joined[:, head * DH : (head + 1) * DH])


def project(x, w, down, up, cosine, sine, tp_count, rotated_heads):
    rows, width = x.shape
    heads = w.shape[1] // DH
    pair = 2
    own = rows // tp_count
    return pl.pallas_call(
        functools.partial(project_kernel, rotated_heads // pair),
        grid=(heads // pair,),
        in_specs=[
            pl.BlockSpec((rows, width), lambda i: (0, 0)),
            pl.BlockSpec((width, pair * DH), lambda i: (0, i)),
            pl.BlockSpec(down.shape, lambda i: (0, 0)),
            pl.BlockSpec((up.shape[0], pair * DH), lambda i: (0, i)),
            pl.BlockSpec((rows, DH), lambda i: (0, 0)),
            pl.BlockSpec((rows, DH), lambda i: (0, 0)),
        ],
        out_specs=pl.BlockSpec((tp_count, pair, own, DH), lambda i: (0, i, 0, 0)),
        out_shape=jax.ShapeDtypeStruct((tp_count, heads, own, DH), jnp.bfloat16),
        scratch_shapes=[pltpu.VMEM((rows, down.shape[1]), jnp.bfloat16)],
        name="project",
    )(x, w, down, up, cosine, sine)


def select_kernel(index_ref, in_ref, out_ref):
    @pl.loop(0, out_ref.shape[0])
    def _(slot):
        out_ref[slot] = in_ref[index_ref[slot]]


def select(index, slabs):
    return pl.pallas_call(
        select_kernel,
        in_specs=[pl.BlockSpec(memory_space=pltpu.SMEM), pl.BlockSpec(memory_space=pltpu.VMEM)],
        out_specs=pl.BlockSpec(memory_space=pltpu.VMEM),
        out_shape=jax.ShapeDtypeStruct((index.shape[0],) + slabs.shape[1:], slabs.dtype),
        name="select_heads",
    )(index, slabs)


def merge_kernel(index_ref, in_ref, out_ref):
    for head in range(in_ref.shape[0]):
        out_ref[:, head * DH : (head + 1) * DH] = in_ref[index_ref[head]]


def merge(index, slabs):
    heads, rows, _ = slabs.shape
    return pl.pallas_call(
        merge_kernel,
        in_specs=[pl.BlockSpec(memory_space=pltpu.SMEM), pl.BlockSpec(memory_space=pltpu.VMEM)],
        out_specs=pl.BlockSpec(memory_space=pltpu.VMEM),
        out_shape=jax.ShapeDtypeStruct((rows, heads * DH), slabs.dtype),
        name="merge_heads",
    )(index, slabs)


def attend_kernel(heads, first_ref, place_ref, q_ref, kv_ref, begin_ref, out_ref):
    step = pl.program_id(0)
    chunks, _, _, own, _ = kv_ref.shape
    block = chunks * own
    rows = heads * own
    q = q_ref[0, :heads].reshape(rows, DH)
    place = place_ref[step]
    begins = jnp.concatenate([begin_ref[...]] * heads, 0)
    places = place + lax.broadcasted_iota(jnp.int32, (own, 1), 0)
    places = jnp.concatenate([places] * heads, 0)
    factor = (DH**-0.5) * LOG2_E

    def body(index, carry):
        top, total, acc = carry
        keys = kv_ref[:, index, 0].reshape(block, DH)
        values = kv_ref[:, index, 1].reshape(block, DH)
        scores = lax.dot_general(
            q, keys, (((1,), (1,)), ((), ())), preferred_element_type=jnp.float32
        )
        at = index * block + lax.broadcasted_iota(jnp.int32, (1, block), 1)
        scores = jnp.where((at <= places) & (at >= begins), scores, NEG_BIG)
        new_top = jnp.maximum(top, jnp.max(scores, 1, keepdims=True))
        shrink = jnp.exp2((top - new_top) * factor)
        powers = jnp.exp2((scores - new_top) * factor)
        total = total * shrink + jnp.sum(powers, 1, keepdims=True)
        acc = acc * shrink + jnp.dot(
            powers.astype(jnp.bfloat16), values, preferred_element_type=jnp.float32
        )
        return new_top, total, acc

    last = place // block
    start = (
        jnp.full((rows, 1), NEG_BIG, jnp.float32),
        jnp.zeros((rows, 1), jnp.float32),
        jnp.zeros((rows, DH), jnp.float32),
    )
    carry = body(last, start)
    top, total, acc = lax.fori_loop(first_ref[step] // block, last, body, carry)
    out_ref[0] = (acc / total).astype(jnp.bfloat16).reshape(heads, own, DH)


def attend(first, place, q, kv, begins, heads):
    steps, slabs, own, _ = q.shape
    return pl.pallas_call(
        functools.partial(attend_kernel, heads),
        grid_spec=pltpu.PrefetchScalarGridSpec(
            num_scalar_prefetch=2,
            grid=(steps,),
            in_specs=[
                pl.BlockSpec((1, slabs, own, DH), lambda i, *_: (i, 0, 0, 0)),
                pl.BlockSpec(kv.shape, lambda i, *_: (0,) * 5),
                pl.BlockSpec((own, 1), lambda i, *_: (i, 0)),
            ],
            out_specs=pl.BlockSpec((1, heads, own, DH), lambda i, *_: (i, 0, 0, 0)),
        ),
        out_shape=jax.ShapeDtypeStruct((steps, heads, own, DH), jnp.bfloat16),
        name="attend",
    )(first, place, q, kv, begins)


def head_tables(query_to_key_head, tp_count, seq_count):
    heads = jnp.arange(H, dtype=jnp.int32)
    same = query_to_key_head[:, None] == query_to_key_head[None, :]
    earlier = heads[None, :] < heads[:, None]
    slot = GROUP * query_to_key_head + jnp.sum((same & earlier).astype(jnp.int32), 1)
    order = jnp.sum(jnp.where(slot[None, :] == heads[:, None], heads[None, :], 0), 1)
    q_per, kv_per = H // tp_count, KV // tp_count
    local = q_per + 2 * kv_per
    here = H // seq_count
    q_index = (order // q_per * local + order % q_per).reshape(seq_count, here)
    kv_head = jnp.arange(seq_count, dtype=jnp.int32) * here // GROUP
    k_index = kv_head // kv_per * local + q_per + kv_head % kv_per
    index = jnp.concatenate([q_index, k_index[:, None], k_index[:, None] + kv_per], 1)
    return index.reshape(-1).astype(jnp.int32), slot.astype(jnp.int32)


def per_device(
    tokens,
    joined_projection_weight,
    adapter_down_weight,
    adapter_up_weight,
    document_index,
    query_to_key_head,
):
    tp_count = lax.axis_size("tp")
    seq_count = lax.axis_size("seq")
    tp_rank = lax.axis_index("tp")
    seq_rank = lax.axis_index("seq")
    own = tokens.shape[0]
    block = own * tp_count
    here = H // seq_count
    q_per, kv_per = H // tp_count, KV // tp_count

    index, slot = head_tables(query_to_key_head, tp_count, seq_count)
    places = (seq_rank * block + jnp.arange(block, dtype=jnp.int32)).astype(jnp.float32)
    cosine, sine = rope_tables(places)
    first_place = jnp.arange(seq_count, dtype=jnp.int32) * block + tp_rank * own
    all_places = jnp.arange(document_index.shape[0], dtype=jnp.int32)
    starts_here = jnp.concatenate(
        [jnp.ones((1,), jnp.bool_), document_index[1:] != document_index[:-1]]
    )
    begin = lax.cummax(jnp.where(starts_here, all_places, 0))
    begin = lax.dynamic_slice_in_dim(
        begin.reshape(seq_count, tp_count, own), tp_rank, 1, 1
    ).reshape(seq_count, own)

    rows = lax.all_gather(tokens, "tp", axis=0, tiled=True)
    heads = project(
        rows, joined_projection_weight, adapter_down_weight, adapter_up_weight,
        cosine, sine, tp_count, q_per + kv_per,
    )
    heads = lax.all_to_all(heads, "tp", split_axis=0, concat_axis=0, tiled=True)
    sent = select(index, heads.reshape(-1, own, DH)).reshape(seq_count, here + 2, own, DH)
    held = lax.all_to_all(sent, "seq", split_axis=0, concat_axis=0, tiled=True)
    kv = lax.all_gather(held[:, here:], "tp", axis=0)
    context = attend(
        begin[:, 0], first_place, held, kv, begin.reshape(seq_count * own, 1), here
    )
    context = lax.all_to_all(context, "seq", split_axis=0, concat_axis=0, tiled=True)
    return merge(slot, context.reshape(H, own, DH))


def solution(mesh):
    return jax.shard_map(
        per_device,
        mesh=mesh,
        in_specs=(P(("seq", "tp"), None), P(None, "tp"), P(), P(None, "tp"), P(), P()),
        out_specs=P(("seq", "tp"), None),
        check_vma=False,
    )
```

```python
import functools

import jax
import jax.numpy as jnp
from jax import lax
from jax.experimental import pallas as pl
from jax.experimental.pallas import tpu as pltpu
from jax.sharding import PartitionSpec as P

H = 32
KV = 8
DH = 128
GROUP = H // KV

ADAPTER_SCALE = 0.5
THETA = 500000.0
NEG_BIG = -1e30
LOG2_E = 1.4426950408889634


def rope_tables(places):
    half = DH // 2
    frequency = THETA ** (-(jnp.arange(half, dtype=jnp.float32) * 2.0) / DH)
    angles = places[:, None] * frequency[None, :]
    cosine, sine = jnp.cos(angles), jnp.sin(angles)
    return jnp.concatenate([cosine, cosine], 1), jnp.concatenate([-sine, sine], 1)


MESH = pl.DeviceIdType.MESH


def front_kernel(
    rotated_pairs, here, index_ref, tokens_ref, w_ref, down_ref, up_ref, cos_ref, sin_ref,
    q_ref, kv_ref,
    x_all, w_all, stage, landed, sent, mid_ref,
    w_sem, local_sem, send_sem, x_sem, land_sem, q_sem, kv_sem, spread_sem,
):
    tp = lax.axis_index("tp")
    seq = lax.axis_index("seq")
    chips, _, own, _ = x_all.shape
    halves, half = 2, own // 2
    tp_count, seq_count = 2 * chips, q_ref.shape[0]
    steps = w_all.shape[0]
    wide = w_all.shape[2]
    pair = wide // DH
    chip, core = tp // 2, tp % 2
    partner = chip * 2 + (1 - core)
    sends = []

    def send(src, dst, sem, axis, target):
        copy = pltpu.make_async_remote_copy(
            src_ref=src, dst_ref=dst, send_sem=send_sem.at[len(sends)], recv_sem=sem,
            device_id={axis: target}, device_id_type=MESH,
        )
        copy.start()
        sends.append(copy)

    def arrived(dst, sem, axis, source):
        pltpu.make_async_remote_copy(
            src_ref=dst, dst_ref=dst, send_sem=send_sem.at[0], recv_sem=sem,
            device_id={axis: source}, device_id_type=MESH,
        ).wait_recv()

    def weight_copy(step):
        return pltpu.make_async_copy(
            w_ref.at[:, pl.ds(pl.multiple_of(step * wide, wide), wide)], w_all.at[step], w_sem.at[step]
        )

    own_copy = pltpu.make_async_copy(tokens_ref, x_all.at[chip, core], local_sem.at[0])
    own_copy.start()
    for step in range(steps):
        weight_copy(step).start()

    barrier = pltpu.get_barrier_semaphore()
    for k in range(1, tp_count):
        pl.semaphore_signal(
            barrier, inc=1, device_id={"tp": (tp + k) % tp_count}, device_id_type=MESH
        )
    for k in range(1, seq_count):
        pl.semaphore_signal(
            barrier, inc=1, device_id={"seq": (seq + k) % seq_count}, device_id_type=MESH
        )
    pl.semaphore_wait(barrier, tp_count - 1 + seq_count - 1)

    def rows_of(h):
        return pl.ds(h * half, half)

    others = [(chip + k) % chips for k in range(1, chips)]
    for h in range(halves):
        for other in others:
            send(
                tokens_ref.at[rows_of(h)], x_all.at[chip, core, rows_of(h)],
                x_sem.at[chip, core, h], "tp", other * 2 + core,
            )
        send(
            tokens_ref.at[rows_of(h)], x_all.at[chip, core, rows_of(h)],
            x_sem.at[chip, core, h], "tp", partner,
        )

    def compute(where, low, count, first):
        rows = pl.ds(low, count)
        x = x_all[where, :, rows, :].reshape(2 * count, x_all.shape[3])
        mid_ref[pl.ds(0, 2 * count)] = jnp.dot(
            x, down_ref[...], preferred_element_type=jnp.float32
        ).astype(jnp.bfloat16)

        @pl.loop(0, steps)
        def _(step):
            if first:
                weight_copy(step).wait()
            x = x_all[where, :, rows, :].reshape(2 * count, x_all.shape[3])
            joined = jnp.dot(x, w_all[step], preferred_element_type=jnp.float32)
            joined = joined + ADAPTER_SCALE * jnp.dot(
                mid_ref[pl.ds(0, 2 * count)], up_ref[step], preferred_element_type=jnp.float32
            )
            kind = step // rotated_pairs
            cosine = cos_ref[kind, where, :, rows, :].reshape(2 * count, DH)
            sine = sin_ref[kind, where, :, rows, :].reshape(2 * count, DH)
            for head in range(pair):
                part = joined[:, head * DH : (head + 1) * DH]
                part = part * cosine + pltpu.roll(part, DH // 2, 1) * sine
                part = part.astype(jnp.bfloat16)
                for k in range(2):
                    stage[where, k, step * pair + head, rows] = part[k * count : (k + 1) * count]

    def give(where, k, h, target):
        send(
            stage.at[where, k, :, rows_of(h)], landed.at[tp, :, rows_of(h)],
            land_sem.at[tp, h], "tp", target,
        )

    own_copy.wait()
    for h in range(halves):
        arrived(x_all.at[chip, 1 - core, rows_of(h)], x_sem.at[chip, 1 - core, h], "tp", partner)
    compute(chip, 0, own, True)
    keep = pltpu.make_async_copy(stage.at[chip, core], landed.at[tp], local_sem.at[0])
    keep.start()
    for h in range(halves):
        give(chip, 1 - core, h, partner)
    for h in range(halves):
        for other in others:
            block = x_all.at[other, core, rows_of(h)]
            arrived(block, x_sem.at[other, core, h], "tp", other * 2 + core)
            send(block, block, x_sem.at[other, core, h], "tp", partner)
        for other in others:
            arrived(
                x_all.at[other, 1 - core, rows_of(h)], x_sem.at[other, 1 - core, h], "tp", partner
            )
            compute(other, h * half, half, False)
            for k in range(2):
                give(other, k, h, other * 2 + k)
    keep.wait()
    for k in range(1, tp_count):
        source = (tp + k) % tp_count
        for h in range(halves):
            arrived(landed.at[source, :, rows_of(h)], land_sem.at[source, h], "tp", source)

    local = landed.shape[1]
    slabs = here + 2

    def pick(slot):
        flat = index_ref[slot]
        sent[slot // slabs, slot % slabs] = landed[flat // local, flat % local]

    @pl.loop(0, seq_count)
    def _(j):
        for slot in range(here, slabs):
            pick(j * slabs + slot)

    near = [(seq + k) % seq_count for k in range(1, seq_count)]
    for j in near:
        send(sent.at[j, pl.ds(here, 2)], kv_ref.at[tp, seq], kv_sem.at[seq], "seq", j)

    @pl.loop(0, seq_count)
    def _(j):
        for slot in range(here):
            pick(j * slabs + slot)

    for j in near:
        send(sent.at[j, pl.ds(0, here)], q_ref.at[seq], q_sem.at[seq], "seq", j)
    mine_kv = pltpu.make_async_copy(
        sent.at[seq, pl.ds(here, 2)], kv_ref.at[tp, seq], local_sem.at[0]
    )
    mine_q = pltpu.make_async_copy(sent.at[seq, pl.ds(0, here)], q_ref.at[seq], local_sem.at[1])
    mine_kv.start()
    mine_q.start()
    mine_kv.wait()
    for n, source in enumerate([seq] + near[::-1]):
        block = kv_ref.at[tp, source]
        if n:
            arrived(block, kv_sem.at[source], "seq", source)
        for k in range(1, tp_count):
            send(block, block, spread_sem.at[tp, source], "tp", (tp + k) % tp_count)
    mine_q.wait()
    for source in near:
        arrived(q_ref.at[source], q_sem.at[source], "seq", source)
    for k in range(1, tp_count):
        source = (tp + k) % tp_count
        for s in range(seq_count):
            arrived(kv_ref.at[source, s], spread_sem.at[source, s], "tp", source)
    for copy in sends:
        copy.wait_send()


def front(index, tokens, w, down, up, cosine, sine, tp_count, seq_count, rotated_heads):
    own, width = tokens.shape
    heads = w.shape[1] // DH
    pair = 2
    steps = heads // pair
    chips = tp_count // 2
    here = H // seq_count
    rank = down.shape[1]
    up = up.reshape(rank, steps, pair * DH).transpose(1, 0, 2)
    vmem = pl.BlockSpec(memory_space=pltpu.VMEM)
    anywhere = pl.BlockSpec(memory_space=pl.ANY)
    count = (
        2 * chips + 2 + 2 * (chips - 1) * 3 + 2 * (seq_count - 1) + seq_count * (tp_count - 1)
    )
    bf16 = jnp.bfloat16
    return pl.pallas_call(
        functools.partial(front_kernel, rotated_heads // pair, here),
        in_specs=[pl.BlockSpec(memory_space=pltpu.SMEM), anywhere, anywhere, vmem, vmem, vmem, vmem],
        out_specs=[anywhere, anywhere],
        out_shape=[
            jax.ShapeDtypeStruct((seq_count, here, own, DH), bf16),
            jax.ShapeDtypeStruct((tp_count, seq_count, 2, own, DH), bf16),
        ],
        scratch_shapes=[
            pltpu.VMEM((chips, 2, own, width), bf16),
            pltpu.VMEM((steps, width, pair * DH), bf16),
            pltpu.VMEM((chips, 2, heads, own, DH), bf16),
            pltpu.VMEM((tp_count, heads, own, DH), bf16),
            pltpu.VMEM((seq_count, here + 2, own, DH), bf16),
            pltpu.VMEM((2 * own, rank), bf16),
            pltpu.SemaphoreType.DMA((steps,)),
            pltpu.SemaphoreType.DMA((2,)),
            pltpu.SemaphoreType.DMA((count,)),
            pltpu.SemaphoreType.DMA((chips, 2, 2)),
            pltpu.SemaphoreType.DMA((tp_count, 2)),
            pltpu.SemaphoreType.DMA((seq_count,)),
            pltpu.SemaphoreType.DMA((seq_count,)),
            pltpu.SemaphoreType.DMA((tp_count, seq_count)),
        ],
        compiler_params=pltpu.CompilerParams(collective_id=0, has_side_effects=True),
        name="front",
    )(index, tokens, w, down, up, cosine, sine)


def merge_kernel(index_ref, in_ref, out_ref):
    for head in range(in_ref.shape[0]):
        out_ref[:, head * DH : (head + 1) * DH] = in_ref[index_ref[head]]


def merge(index, slabs):
    heads, rows, _ = slabs.shape
    return pl.pallas_call(
        merge_kernel,
        in_specs=[pl.BlockSpec(memory_space=pltpu.SMEM), pl.BlockSpec(memory_space=pltpu.VMEM)],
        out_specs=pl.BlockSpec(memory_space=pltpu.VMEM),
        out_shape=jax.ShapeDtypeStruct((rows, heads * DH), slabs.dtype),
        name="merge_heads",
    )(index, slabs)


def attend_kernel(heads, first_ref, place_ref, q_ref, kv_ref, begin_ref, out_ref):
    step = pl.program_id(0)
    chunks, _, _, own, _ = kv_ref.shape
    block = chunks * own
    rows = heads * own
    q = q_ref[0, :heads].reshape(rows, DH)
    place = place_ref[step]
    begins = jnp.concatenate([begin_ref[...]] * heads, 0)
    places = place + lax.broadcasted_iota(jnp.int32, (own, 1), 0)
    places = jnp.concatenate([places] * heads, 0)
    factor = (DH**-0.5) * LOG2_E

    def body(index, carry):
        top, total, acc = carry
        keys = kv_ref[:, index, 0].reshape(block, DH)
        values = kv_ref[:, index, 1].reshape(block, DH)
        scores = lax.dot_general(
            q, keys, (((1,), (1,)), ((), ())), preferred_element_type=jnp.float32
        )
        at = index * block + lax.broadcasted_iota(jnp.int32, (1, block), 1)
        scores = jnp.where((at <= places) & (at >= begins), scores, NEG_BIG)
        new_top = jnp.maximum(top, jnp.max(scores, 1, keepdims=True))
        shrink = jnp.exp2((top - new_top) * factor)
        powers = jnp.exp2((scores - new_top) * factor)
        total = total * shrink + jnp.sum(powers, 1, keepdims=True)
        acc = acc * shrink + jnp.dot(
            powers.astype(jnp.bfloat16), values, preferred_element_type=jnp.float32
        )
        return new_top, total, acc

    last = place // block
    start = (
        jnp.full((rows, 1), NEG_BIG, jnp.float32),
        jnp.zeros((rows, 1), jnp.float32),
        jnp.zeros((rows, DH), jnp.float32),
    )
    carry = body(last, start)
    top, total, acc = lax.fori_loop(first_ref[step] // block, last, body, carry)
    out_ref[0] = (acc / total).astype(jnp.bfloat16).reshape(heads, own, DH)


def attend(first, place, q, kv, begins, heads):
    steps, slabs, own, _ = q.shape
    return pl.pallas_call(
        functools.partial(attend_kernel, heads),
        grid_spec=pltpu.PrefetchScalarGridSpec(
            num_scalar_prefetch=2,
            grid=(steps,),
            in_specs=[
                pl.BlockSpec((1, slabs, own, DH), lambda i, *_: (i, 0, 0, 0)),
                pl.BlockSpec(kv.shape, lambda i, *_: (0,) * 5),
                pl.BlockSpec((own, 1), lambda i, *_: (i, 0)),
            ],
            out_specs=pl.BlockSpec((1, heads, own, DH), lambda i, *_: (i, 0, 0, 0)),
        ),
        out_shape=jax.ShapeDtypeStruct((steps, heads, own, DH), jnp.bfloat16),
        name="attend",
    )(first, place, q, kv, begins)


def head_tables(query_to_key_head, tp_count, seq_count):
    heads = jnp.arange(H, dtype=jnp.int32)
    same = query_to_key_head[:, None] == query_to_key_head[None, :]
    earlier = heads[None, :] < heads[:, None]
    slot = GROUP * query_to_key_head + jnp.sum((same & earlier).astype(jnp.int32), 1)
    order = jnp.sum(jnp.where(slot[None, :] == heads[:, None], heads[None, :], 0), 1)
    q_per, kv_per = H // tp_count, KV // tp_count
    local = q_per + 2 * kv_per
    here = H // seq_count
    q_index = (order // q_per * local + order % q_per).reshape(seq_count, here)
    kv_head = jnp.arange(seq_count, dtype=jnp.int32) * here // GROUP
    k_index = kv_head // kv_per * local + q_per + kv_head % kv_per
    index = jnp.concatenate([q_index, k_index[:, None], k_index[:, None] + kv_per], 1)
    return index.reshape(-1).astype(jnp.int32), slot.astype(jnp.int32)


def per_device(
    tokens,
    joined_projection_weight,
    adapter_down_weight,
    adapter_up_weight,
    document_index,
    query_to_key_head,
):
    tp_count = lax.axis_size("tp")
    seq_count = lax.axis_size("seq")
    tp_rank = lax.axis_index("tp")
    seq_rank = lax.axis_index("seq")
    own = tokens.shape[0]
    block = own * tp_count
    here = H // seq_count
    q_per, kv_per = H // tp_count, KV // tp_count

    index, slot = head_tables(query_to_key_head, tp_count, seq_count)
    places = (seq_rank * block + jnp.arange(block, dtype=jnp.int32)).astype(jnp.float32)
    cosine, sine = rope_tables(places)
    first_place = jnp.arange(seq_count, dtype=jnp.int32) * block + tp_rank * own
    all_places = jnp.arange(document_index.shape[0], dtype=jnp.int32)
    starts_here = jnp.concatenate(
        [jnp.ones((1,), jnp.bool_), document_index[1:] != document_index[:-1]]
    )
    begin = lax.cummax(jnp.where(starts_here, all_places, 0))
    begin = lax.dynamic_slice_in_dim(
        begin.reshape(seq_count, tp_count, own), tp_rank, 1, 1
    ).reshape(seq_count, own)

    table = (1, tp_count // 2, 2, own, DH)
    cosine = jnp.concatenate([cosine.reshape(table), jnp.ones(table, jnp.float32)])
    sine = jnp.concatenate([sine.reshape(table), jnp.zeros(table, jnp.float32)])
    held, kv = front(
        index, tokens, joined_projection_weight, adapter_down_weight, adapter_up_weight,
        cosine, sine, tp_count, seq_count, q_per + kv_per,
    )
    context = attend(
        begin[:, 0], first_place, held, kv, begin.reshape(seq_count * own, 1), here
    )
    context = lax.all_to_all(context, "seq", split_axis=0, concat_axis=0, tiled=True)
    return merge(slot, context.reshape(H, own, DH))


def solution(mesh):
    return jax.shard_map(
        per_device,
        mesh=mesh,
        in_specs=(P(("seq", "tp"), None), P(None, "tp"), P(), P(None, "tp"), P(), P()),
        out_specs=P(("seq", "tp"), None),
        check_vma=False,
    )
```

```python
import functools

import jax
import jax.numpy as jnp
from jax import lax
from jax.experimental import pallas as pl
from jax.experimental.pallas import tpu as pltpu
from jax.sharding import PartitionSpec as P

H = 32
KV = 8
DH = 128
GROUP = H // KV

ADAPTER_SCALE = 0.5
THETA = 500000.0
NEG_BIG = -1e30
LOG2_E = 1.4426950408889634


def rope_tables(places):
    half = DH // 2
    frequency = THETA ** (-(jnp.arange(half, dtype=jnp.float32) * 2.0) / DH)
    angles = places[:, None] * frequency[None, :]
    cosine, sine = jnp.cos(angles), jnp.sin(angles)
    return jnp.concatenate([cosine, cosine], 1), jnp.concatenate([-sine, sine], 1)


MESH = pl.DeviceIdType.MESH


def front_kernel(
    rotated_pairs, here, index_ref, tokens_ref, w_ref, down_ref, up_ref, cos_ref, sin_ref,
    q_ref, kv_ref,
    x_all, w_all, stage, landed, sent, mid_ref,
    w_sem, local_sem, send_sem, x_sem, land_sem, q_sem, kv_sem, spread_sem,
):
    tp = lax.axis_index("tp")
    seq = lax.axis_index("seq")
    chips, _, own, _ = x_all.shape
    halves, half = 2, own // 2
    tp_count, seq_count = 2 * chips, q_ref.shape[0]
    steps = w_all.shape[0]
    wide = w_all.shape[2]
    pair = wide // DH
    chip, core = tp // 2, tp % 2
    partner = chip * 2 + (1 - core)
    sends = []

    def send(src, dst, sem, axis, target):
        copy = pltpu.make_async_remote_copy(
            src_ref=src, dst_ref=dst, send_sem=send_sem.at[len(sends)], recv_sem=sem,
            device_id={axis: target}, device_id_type=MESH,
        )
        copy.start()
        sends.append(copy)

    def arrived(dst, sem, axis, source):
        pltpu.make_async_remote_copy(
            src_ref=dst, dst_ref=dst, send_sem=send_sem.at[0], recv_sem=sem,
            device_id={axis: source}, device_id_type=MESH,
        ).wait_recv()

    def weight_copy(step):
        return pltpu.make_async_copy(
            w_ref.at[:, pl.ds(pl.multiple_of(step * wide, wide), wide)], w_all.at[step], w_sem.at[step]
        )

    own_copy = pltpu.make_async_copy(tokens_ref, x_all.at[chip, core], local_sem.at[0])
    own_copy.start()
    for step in range(steps):
        weight_copy(step).start()

    barrier = pltpu.get_barrier_semaphore()
    for k in range(1, tp_count):
        pl.semaphore_signal(
            barrier, inc=1, device_id={"tp": (tp + k) % tp_count}, device_id_type=MESH
        )
    for k in range(1, seq_count):
        pl.semaphore_signal(
            barrier, inc=1, device_id={"seq": (seq + k) % seq_count}, device_id_type=MESH
        )
    pl.semaphore_wait(barrier, tp_count - 1 + seq_count - 1)

    def rows_of(h):
        return pl.ds(h * half, half)

    others = [(chip + k) % chips for k in range(1, chips)]
    for h in range(halves):
        for other in others:
            send(
                tokens_ref.at[rows_of(h)], x_all.at[chip, core, rows_of(h)],
                x_sem.at[chip, core, h], "tp", other * 2 + core,
            )
        send(
            tokens_ref.at[rows_of(h)], x_all.at[chip, core, rows_of(h)],
            x_sem.at[chip, core, h], "tp", partner,
        )

    def compute(where, low, count, first):
        rows = pl.ds(low, count)
        x = x_all[where, :, rows, :].reshape(2 * count, x_all.shape[3])
        mid_ref[pl.ds(0, 2 * count)] = lax.dot_general(
            x, down_ref[...], (((1,), (1,)), ((), ())), preferred_element_type=jnp.float32
        ).astype(jnp.bfloat16)

        @pl.loop(0, steps)
        def _(step):
            if first:
                weight_copy(step).wait()
            x = x_all[where, :, rows, :].reshape(2 * count, x_all.shape[3])
            joined = jnp.dot(x, w_all[step], preferred_element_type=jnp.float32)
            joined = joined + ADAPTER_SCALE * jnp.dot(
                mid_ref[pl.ds(0, 2 * count)], up_ref[:, pl.ds(pl.multiple_of(step * wide, wide), wide)],
                preferred_element_type=jnp.float32
            )
            kind = step // rotated_pairs
            cosine = cos_ref[kind, where, :, rows, :].reshape(2 * count, DH)
            sine = sin_ref[kind, where, :, rows, :].reshape(2 * count, DH)
            for head in range(pair):
                part = joined[:, head * DH : (head + 1) * DH]
                part = part * cosine + pltpu.roll(part, DH // 2, 1) * sine
                part = part.astype(jnp.bfloat16)
                for k in range(2):
                    stage[where, k, step * pair + head, rows] = part[k * count : (k + 1) * count]

    def give(where, k, h, target):
        send(
            stage.at[where, k, :, rows_of(h)], landed.at[tp, :, rows_of(h)],
            land_sem.at[tp, h], "tp", target,
        )

    own_copy.wait()
    for h in range(halves):
        arrived(x_all.at[chip, 1 - core, rows_of(h)], x_sem.at[chip, 1 - core, h], "tp", partner)
    compute(chip, 0, own, True)
    keep = pltpu.make_async_copy(stage.at[chip, core], landed.at[tp], local_sem.at[0])
    keep.start()
    for h in range(halves):
        give(chip, 1 - core, h, partner)
    for h in range(halves):
        for other in others:
            block = x_all.at[other, core, rows_of(h)]
            arrived(block, x_sem.at[other, core, h], "tp", other * 2 + core)
            send(block, block, x_sem.at[other, core, h], "tp", partner)
        for other in others:
            arrived(
                x_all.at[other, 1 - core, rows_of(h)], x_sem.at[other, 1 - core, h], "tp", partner
            )
            compute(other, h * half, half, False)
            for k in range(2):
                give(other, k, h, other * 2 + k)
    keep.wait()
    for k in range(1, tp_count):
        source = (tp + k) % tp_count
        for h in range(halves):
            arrived(landed.at[source, :, rows_of(h)], land_sem.at[source, h], "tp", source)

    q_per = H // tp_count
    kv_per = KV // tp_count

    @pl.loop(0, seq_count)
    def _(j):
        kv_head = j * here // GROUP
        for k in range(2):
            sent[j, here + k] = landed[
                kv_head // kv_per, q_per + k * kv_per + kv_head % kv_per
            ]

    near = [(seq + k) % seq_count for k in range(1, seq_count)]
    for j in near:
        send(sent.at[j, pl.ds(here, 2)], kv_ref.at[tp, seq], kv_sem.at[seq], "seq", j)

    @pl.loop(0, seq_count)
    def _(j):
        for k in range(here):
            head = index_ref[j * here + k]
            sent[j, k] = landed[head // q_per, head % q_per]

    for j in near:
        send(sent.at[j, pl.ds(0, here)], q_ref.at[seq], q_sem.at[seq], "seq", j)
    mine_kv = pltpu.make_async_copy(
        sent.at[seq, pl.ds(here, 2)], kv_ref.at[tp, seq], local_sem.at[0]
    )
    mine_q = pltpu.make_async_copy(sent.at[seq, pl.ds(0, here)], q_ref.at[seq], local_sem.at[1])
    mine_kv.start()
    mine_q.start()
    mine_kv.wait()
    for n, source in enumerate([seq] + near[::-1]):
        block = kv_ref.at[tp, source]
        if n:
            arrived(block, kv_sem.at[source], "seq", source)
        for k in range(1, tp_count):
            send(block, block, spread_sem.at[tp, source], "tp", (tp + k) % tp_count)
    mine_q.wait()
    for source in near:
        arrived(q_ref.at[source], q_sem.at[source], "seq", source)
    for k in range(1, tp_count):
        source = (tp + k) % tp_count
        for s in range(seq_count):
            arrived(kv_ref.at[source, s], spread_sem.at[source, s], "tp", source)
    for copy in sends:
        copy.wait_send()


def front(index, tokens, w, down, up, cosine, sine, tp_count, seq_count, rotated_heads):
    own, width = tokens.shape
    heads = w.shape[1] // DH
    pair = 2
    steps = heads // pair
    chips = tp_count // 2
    here = H // seq_count
    rank = down.shape[1]
    vmem = pl.BlockSpec(memory_space=pltpu.VMEM)
    anywhere = pl.BlockSpec(memory_space=pl.ANY)
    count = (
        2 * chips + 2 + 2 * (chips - 1) * 3 + 2 * (seq_count - 1) + seq_count * (tp_count - 1)
    )
    bf16 = jnp.bfloat16
    return pl.pallas_call(
        functools.partial(front_kernel, rotated_heads // pair, here),
        in_specs=[pl.BlockSpec(memory_space=pltpu.SMEM), anywhere, anywhere, vmem, vmem, vmem, vmem],
        out_specs=[anywhere, anywhere],
        out_shape=[
            jax.ShapeDtypeStruct((seq_count, here, own, DH), bf16),
            jax.ShapeDtypeStruct((tp_count, seq_count, 2, own, DH), bf16),
        ],
        scratch_shapes=[
            pltpu.VMEM((chips, 2, own, width), bf16),
            pltpu.VMEM((steps, width, pair * DH), bf16),
            pltpu.VMEM((chips, 2, heads, own, DH), bf16),
            pltpu.VMEM((tp_count, heads, own, DH), bf16),
            pltpu.VMEM((seq_count, here + 2, own, DH), bf16),
            pltpu.VMEM((2 * own, rank), bf16),
            pltpu.SemaphoreType.DMA((steps,)),
            pltpu.SemaphoreType.DMA((2,)),
            pltpu.SemaphoreType.DMA((count,)),
            pltpu.SemaphoreType.DMA((chips, 2, 2)),
            pltpu.SemaphoreType.DMA((tp_count, 2)),
            pltpu.SemaphoreType.DMA((seq_count,)),
            pltpu.SemaphoreType.DMA((seq_count,)),
            pltpu.SemaphoreType.DMA((tp_count, seq_count)),
        ],
        compiler_params=pltpu.CompilerParams(collective_id=0, has_side_effects=True),
        name="front",
    )(index, tokens, w, down.T, up, cosine, sine)


def finish_kernel(slot_ref, in_ref, out_ref, landed, send_sem, land_sem, local_sem):
    seq = lax.axis_index("seq")
    seq_count, here, _, _ = landed.shape
    own_copy = pltpu.make_async_copy(in_ref.at[seq], landed.at[seq], local_sem.at[0])
    own_copy.start()
    near = [(seq + k) % seq_count for k in range(1, seq_count)]
    barrier = pltpu.get_barrier_semaphore()
    for j in near:
        pl.semaphore_signal(barrier, inc=1, device_id={"seq": j}, device_id_type=MESH)
    pl.semaphore_wait(barrier, seq_count - 1)
    sends = []
    for n, j in enumerate(near):
        copy = pltpu.make_async_remote_copy(
            src_ref=in_ref.at[j], dst_ref=landed.at[seq], send_sem=send_sem.at[n],
            recv_sem=land_sem.at[seq], device_id={"seq": j}, device_id_type=MESH,
        )
        copy.start()
        sends.append(copy)
    own_copy.wait()
    for j in near:
        pltpu.make_async_remote_copy(
            src_ref=landed.at[j], dst_ref=landed.at[j], send_sem=send_sem.at[0],
            recv_sem=land_sem.at[j], device_id={"seq": j}, device_id_type=MESH,
        ).wait_recv()
    for head in range(seq_count * here):
        slot = slot_ref[head]
        out_ref[:, head * DH : (head + 1) * DH] = landed[slot // here, slot % here]
    for copy in sends:
        copy.wait_send()


def finish(slot, context):
    seq_count, here, rows, _ = context.shape
    return pl.pallas_call(
        finish_kernel,
        in_specs=[pl.BlockSpec(memory_space=pltpu.SMEM), pl.BlockSpec(memory_space=pl.ANY)],
        out_specs=pl.BlockSpec(memory_space=pltpu.VMEM),
        out_shape=jax.ShapeDtypeStruct((rows, seq_count * here * DH), context.dtype),
        scratch_shapes=[
            pltpu.VMEM(context.shape, context.dtype),
            pltpu.SemaphoreType.DMA((seq_count,)),
            pltpu.SemaphoreType.DMA((seq_count,)),
            pltpu.SemaphoreType.DMA((1,)),
        ],
        compiler_params=pltpu.CompilerParams(collective_id=1, has_side_effects=True),
        name="finish",
    )(slot, context)


def attend_kernel(heads, scalar_ref, q_ref, kv_ref, doc_ref, out_ref):
    step = pl.program_id(0)
    tp = lax.axis_index("tp")
    chunks, _, _, own, _ = kv_ref.shape
    block = chunks * own
    rows = heads * own
    q = q_ref[0, :heads].reshape(rows, DH)
    place = step * block + tp * own
    first = jnp.sum((doc_ref[...] < scalar_ref[place]).astype(jnp.int32))
    docs = doc_ref[pl.ds(step * chunks + tp, 1), :]
    docs = jnp.broadcast_to(docs, (own, own)).T[:, :1]
    docs = jnp.concatenate([docs] * heads, 0)
    places = place + lax.broadcasted_iota(jnp.int32, (own, 1), 0)
    places = jnp.concatenate([places] * heads, 0)
    factor = (DH**-0.5) * LOG2_E

    def body(index, carry):
        top, total, acc = carry
        keys = kv_ref[:, index, 0].reshape(block, DH)
        values = kv_ref[:, index, 1].reshape(block, DH)
        scores = lax.dot_general(
            q, keys, (((1,), (1,)), ((), ())), preferred_element_type=jnp.float32
        )
        at = index * block + lax.broadcasted_iota(jnp.int32, (1, block), 1)
        key_docs = jnp.concatenate(
            [doc_ref[pl.ds(index * chunks + c, 1), :] for c in range(chunks)], 1
        )
        scores = jnp.where((at <= places) & (key_docs == docs), scores, NEG_BIG)
        new_top = jnp.maximum(top, jnp.max(scores, 1, keepdims=True))
        shrink = jnp.exp2((top - new_top) * factor)
        powers = jnp.exp2((scores - new_top) * factor)
        total = total * shrink + jnp.sum(powers, 1, keepdims=True)
        acc = acc * shrink + jnp.dot(
            powers.astype(jnp.bfloat16), values, preferred_element_type=jnp.float32
        )
        return new_top, total, acc

    last = place // block
    start = (
        jnp.full((rows, 1), NEG_BIG, jnp.float32),
        jnp.zeros((rows, 1), jnp.float32),
        jnp.zeros((rows, DH), jnp.float32),
    )
    carry = body(last, start)
    top, total, acc = lax.fori_loop(first // block, last, body, carry)
    out_ref[0] = (acc / total).astype(jnp.bfloat16).reshape(heads, own, DH)


def attend(document_index, q, kv, heads):
    steps, slabs, own, _ = q.shape
    return pl.pallas_call(
        functools.partial(attend_kernel, heads),
        grid_spec=pltpu.PrefetchScalarGridSpec(
            num_scalar_prefetch=1,
            grid=(steps,),
            in_specs=[
                pl.BlockSpec((1, slabs, own, DH), lambda i, *_: (i, 0, 0, 0)),
                pl.BlockSpec(kv.shape, lambda i, *_: (0,) * 5),
                pl.BlockSpec((steps * kv.shape[0], own), lambda i, *_: (0, 0)),
            ],
            out_specs=pl.BlockSpec((1, heads, own, DH), lambda i, *_: (i, 0, 0, 0)),
        ),
        out_shape=jax.ShapeDtypeStruct((steps, heads, own, DH), jnp.bfloat16),
        name="attend",
    )(document_index, q, kv, document_index.reshape(-1, own))


def head_tables(query_to_key_head):
    heads = jnp.arange(H, dtype=jnp.int32)
    same = query_to_key_head[:, None] == query_to_key_head[None, :]
    earlier = heads[None, :] < heads[:, None]
    slot = GROUP * query_to_key_head + jnp.sum((same & earlier).astype(jnp.int32), 1)
    order = jnp.sum(jnp.where(slot[None, :] == heads[:, None], heads[None, :], 0), 1)
    return order.astype(jnp.int32), slot.astype(jnp.int32)


def per_device(
    tokens,
    joined_projection_weight,
    adapter_down_weight,
    adapter_up_weight,
    document_index,
    query_to_key_head,
):
    tp_count = lax.axis_size("tp")
    seq_count = lax.axis_size("seq")
    tp_rank = lax.axis_index("tp")
    seq_rank = lax.axis_index("seq")
    own = tokens.shape[0]
    block = own * tp_count
    here = H // seq_count
    q_per, kv_per = H // tp_count, KV // tp_count

    index, slot = head_tables(query_to_key_head)
    places = (seq_rank * block + jnp.arange(block, dtype=jnp.int32)).astype(jnp.float32)
    cosine, sine = rope_tables(places)
    table = (1, tp_count // 2, 2, own, DH)
    cosine = jnp.concatenate([cosine.reshape(table), jnp.ones(table, jnp.float32)])
    sine = jnp.concatenate([sine.reshape(table), jnp.zeros(table, jnp.float32)])
    held, kv = front(
        index, tokens, joined_projection_weight, adapter_down_weight, adapter_up_weight,
        cosine, sine, tp_count, seq_count, q_per + kv_per,
    )
    context = attend(document_index, held, kv, here)
    return finish(slot, context)


def solution(mesh):
    return jax.shard_map(
        per_device,
        mesh=mesh,
        in_specs=(P(("seq", "tp"), None), P(None, "tp"), P(), P(None, "tp"), P(), P()),
        out_specs=P(("seq", "tp"), None),
        check_vma=False,
    )
```

```python
import functools

import jax
import jax.numpy as jnp
from jax import lax
from jax.experimental import pallas as pl
from jax.experimental.pallas import tpu as pltpu
from jax.sharding import PartitionSpec as P

H = 32
KV = 8
DH = 128
GROUP = H // KV

ADAPTER_SCALE = 0.5
THETA = 500000.0
NEG_BIG = -1e30
LOG2_E = 1.4426950408889634


def rope_tables(places):
    half = DH // 2
    frequency = THETA ** (-(jnp.arange(half, dtype=jnp.float32) * 2.0) / DH)
    angles = places[:, None] * frequency[None, :]
    cosine, sine = jnp.cos(angles), jnp.sin(angles)
    return jnp.concatenate([cosine, cosine], 1), jnp.concatenate([-sine, sine], 1)


MESH = pl.DeviceIdType.MESH


def front_kernel(
    rotated_pairs, here, index_ref, tokens_ref, w_ref, down_ref, up_ref, cos_ref, sin_ref,
    q_ref, kv_ref,
    x_all, w_all, stage, landed_low, landed_high, sent, mid_ref,
    w_sem, local_sem, send_sem, x_sem, land_sem, q_sem, kv_sem, spread_sem,
):
    tp = lax.axis_index("tp")
    seq = lax.axis_index("seq")
    chips, _, own, _ = x_all.shape
    halves, half = 2, own // 2
    tp_count, seq_count = 2 * chips, q_ref.shape[0]
    steps = w_all.shape[0]
    wide = w_all.shape[2]
    pair = wide // DH
    chip, core = tp // 2, tp % 2
    partner = chip * 2 + (1 - core)
    landed = (landed_low, landed_high)
    sends = []

    def send(src, dst, sem, axis, target):
        copy = pltpu.make_async_remote_copy(
            src_ref=src, dst_ref=dst, send_sem=send_sem.at[len(sends)], recv_sem=sem,
            device_id={axis: target}, device_id_type=MESH,
        )
        copy.start()
        sends.append(copy)

    def arrived(dst, sem, axis, source):
        pltpu.make_async_remote_copy(
            src_ref=dst, dst_ref=dst, send_sem=send_sem.at[0], recv_sem=sem,
            device_id={axis: source}, device_id_type=MESH,
        ).wait_recv()

    def weight_copy(step):
        return pltpu.make_async_copy(
            w_ref.at[:, pl.ds(pl.multiple_of(step * wide, wide), wide)], w_all.at[step], w_sem.at[step]
        )

    own_copy = pltpu.make_async_copy(tokens_ref, x_all.at[chip, core], local_sem.at[0])
    own_copy.start()
    for step in range(steps):
        weight_copy(step).start()

    barrier = pltpu.get_barrier_semaphore()
    for k in range(1, tp_count):
        pl.semaphore_signal(
            barrier, inc=1, device_id={"tp": (tp + k) % tp_count}, device_id_type=MESH
        )
    for k in range(1, seq_count):
        pl.semaphore_signal(
            barrier, inc=1, device_id={"seq": (seq + k) % seq_count}, device_id_type=MESH
        )
    pl.semaphore_wait(barrier, tp_count - 1 + seq_count - 1)

    def rows_of(h):
        return pl.ds(h * half, half)

    others = [(chip + k) % chips for k in range(1, chips)]
    for h in range(halves):
        for other in others:
            send(
                tokens_ref.at[rows_of(h)], x_all.at[chip, core, rows_of(h)],
                x_sem.at[chip, core, h], "tp", other * 2 + core,
            )
        send(
            tokens_ref.at[rows_of(h)], x_all.at[chip, core, rows_of(h)],
            x_sem.at[chip, core, h], "tp", partner,
        )

    def compute(where, low, count, first):
        rows = pl.ds(low, count)
        x = x_all[where, :, rows, :].reshape(2 * count, x_all.shape[3])
        mid_ref[pl.ds(0, 2 * count)] = lax.dot_general(
            x, down_ref[...], (((1,), (1,)), ((), ())), preferred_element_type=jnp.float32
        ).astype(jnp.bfloat16)

        @pl.loop(0, steps)
        def _(step):
            if first:
                weight_copy(step).wait()
            x = x_all[where, :, rows, :].reshape(2 * count, x_all.shape[3])
            joined = jnp.dot(x, w_all[step], preferred_element_type=jnp.float32)
            joined = joined + ADAPTER_SCALE * jnp.dot(
                mid_ref[pl.ds(0, 2 * count)], up_ref[:, pl.ds(pl.multiple_of(step * wide, wide), wide)],
                preferred_element_type=jnp.float32
            )
            kind = step // rotated_pairs
            cosine = cos_ref[kind, where, :, rows, :].reshape(2 * count, DH)
            sine = sin_ref[kind, where, :, rows, :].reshape(2 * count, DH)
            for head in range(pair):
                part = joined[:, head * DH : (head + 1) * DH]
                part = part * cosine + pltpu.roll(part, DH // 2, 1) * sine
                part = part.astype(jnp.bfloat16)
                for k in range(2):
                    stage[where, k, step * pair + head, rows] = part[k * count : (k + 1) * count]

    def give(where, k, h, target):
        send(
            stage.at[where, k, :, rows_of(h)], landed[h].at[tp],
            land_sem.at[tp, h], "tp", target,
        )

    own_copy.wait()
    for h in range(halves):
        arrived(x_all.at[chip, 1 - core, rows_of(h)], x_sem.at[chip, 1 - core, h], "tp", partner)
    compute(chip, 0, own, True)
    keeps = [
        pltpu.make_async_copy(
            stage.at[chip, core, :, rows_of(h)], landed[h].at[tp], local_sem.at[5 * h]
        )
        for h in range(halves)
    ]
    for keep in keeps:
        keep.start()
    for h in range(halves):
        give(chip, 1 - core, h, partner)
    for h in range(halves):
        for other in others:
            block = x_all.at[other, core, rows_of(h)]
            arrived(block, x_sem.at[other, core, h], "tp", other * 2 + core)
            send(block, block, x_sem.at[other, core, h], "tp", partner)
        for other in others:
            arrived(
                x_all.at[other, 1 - core, rows_of(h)], x_sem.at[other, 1 - core, h], "tp", partner
            )
            compute(other, h * half, half, False)
            for k in range(2):
                give(other, k, h, other * 2 + k)
    for keep in keeps:
        keep.wait()
    q_per = H // tp_count
    kv_per = KV // tp_count
    near = [(seq + k) % seq_count for k in range(1, seq_count)]
    mine = []

    def hold(src, dst):
        copy = pltpu.make_async_copy(src, dst, local_sem.at[1 + len(mine)])
        copy.start()
        mine.append(copy)

    for h in range(halves):
        rows = rows_of(h)
        for k in range(1, tp_count):
            source = (tp + k) % tp_count
            arrived(landed[h].at[source], land_sem.at[source, h], "tp", source)

        @pl.loop(0, seq_count)
        def _(j):
            kv_head = j * here // GROUP
            for k in range(2):
                sent[j, here + k, rows] = landed[h][
                    kv_head // kv_per, q_per + k * kv_per + kv_head % kv_per
                ]

        for j in near:
            send(
                sent.at[j, pl.ds(here, 2), rows], kv_ref.at[tp, seq, :, rows],
                kv_sem.at[seq, h], "seq", j,
            )

        @pl.loop(0, seq_count)
        def _(j):
            for k in range(here):
                head = index_ref[j * here + k]
                sent[j, k, rows] = landed[h][head // q_per, head % q_per]

        for j in near:
            send(
                sent.at[j, pl.ds(0, here), rows], q_ref.at[seq, :, rows],
                q_sem.at[seq, h], "seq", j,
            )
        hold(sent.at[seq, pl.ds(here, 2), rows], kv_ref.at[tp, seq, :, rows])
        hold(sent.at[seq, pl.ds(0, here), rows], q_ref.at[seq, :, rows])

    for copy in mine:
        copy.wait()
    for h in range(halves):
        for n, source in enumerate([seq] + near[::-1]):
            block = kv_ref.at[tp, source, :, rows_of(h)]
            if n:
                arrived(block, kv_sem.at[source, h], "seq", source)
            for k in range(1, tp_count):
                send(block, block, spread_sem.at[tp, source, h], "tp", (tp + k) % tp_count)
    for h in range(halves):
        for source in near:
            arrived(q_ref.at[source, :, rows_of(h)], q_sem.at[source, h], "seq", source)
        for k in range(1, tp_count):
            source = (tp + k) % tp_count
            for n in range(seq_count):
                arrived(
                    kv_ref.at[source, n, :, rows_of(h)], spread_sem.at[source, n, h], "tp", source
                )
    for copy in sends:
        copy.wait_send()


def front(index, tokens, w, down, up, cosine, sine, tp_count, seq_count, rotated_heads):
    own, width = tokens.shape
    heads = w.shape[1] // DH
    pair = 2
    steps = heads // pair
    chips = tp_count // 2
    here = H // seq_count
    rank = down.shape[1]
    vmem = pl.BlockSpec(memory_space=pltpu.VMEM)
    anywhere = pl.BlockSpec(memory_space=pl.ANY)
    count = (
        2 * chips + 2 + 2 * (chips - 1) * 4 + 4 * (seq_count - 1) + 2 * seq_count * (tp_count - 1)
    )
    bf16 = jnp.bfloat16
    return pl.pallas_call(
        functools.partial(front_kernel, rotated_heads // pair, here),
        in_specs=[pl.BlockSpec(memory_space=pltpu.SMEM), anywhere, anywhere, vmem, vmem, vmem, vmem],
        out_specs=[anywhere, anywhere],
        out_shape=[
            jax.ShapeDtypeStruct((seq_count, here, own, DH), bf16),
            jax.ShapeDtypeStruct((tp_count, seq_count, 2, own, DH), bf16),
        ],
        scratch_shapes=[
            pltpu.VMEM((chips, 2, own, width), bf16),
            pltpu.VMEM((steps, width, pair * DH), bf16),
            pltpu.VMEM((chips, 2, heads, own, DH), bf16),
            pltpu.VMEM((tp_count, heads, own // 2, DH), bf16),
            pltpu.VMEM((tp_count, heads, own // 2, DH), bf16),
            pltpu.VMEM((seq_count, here + 2, own, DH), bf16),
            pltpu.VMEM((2 * own, rank), bf16),
            pltpu.SemaphoreType.DMA((steps,)),
            pltpu.SemaphoreType.DMA((6,)),
            pltpu.SemaphoreType.DMA((count,)),
            pltpu.SemaphoreType.DMA((chips, 2, 2)),
            pltpu.SemaphoreType.DMA((tp_count, 2)),
            pltpu.SemaphoreType.DMA((seq_count, 2)),
            pltpu.SemaphoreType.DMA((seq_count, 2)),
            pltpu.SemaphoreType.DMA((tp_count, seq_count, 2)),
        ],
        compiler_params=pltpu.CompilerParams(collective_id=0, has_side_effects=True),
        name="front",
    )(index, tokens, w, down.T, up, cosine, sine)


def finish_kernel(slot_ref, in_ref, out_ref, landed, send_sem, land_sem, local_sem):
    seq = lax.axis_index("seq")
    seq_count, here, _, _ = landed.shape
    own_copy = pltpu.make_async_copy(in_ref.at[seq], landed.at[seq], local_sem.at[0])
    own_copy.start()
    near = [(seq + k) % seq_count for k in range(1, seq_count)]
    barrier = pltpu.get_barrier_semaphore()
    for j in near:
        pl.semaphore_signal(barrier, inc=1, device_id={"seq": j}, device_id_type=MESH)
    pl.semaphore_wait(barrier, seq_count - 1)
    sends = []
    for n, j in enumerate(near):
        copy = pltpu.make_async_remote_copy(
            src_ref=in_ref.at[j], dst_ref=landed.at[seq], send_sem=send_sem.at[n],
            recv_sem=land_sem.at[seq], device_id={"seq": j}, device_id_type=MESH,
        )
        copy.start()
        sends.append(copy)
    own_copy.wait()
    for j in near:
        pltpu.make_async_remote_copy(
            src_ref=landed.at[j], dst_ref=landed.at[j], send_sem=send_sem.at[0],
            recv_sem=land_sem.at[j], device_id={"seq": j}, device_id_type=MESH,
        ).wait_recv()
    for head in range(seq_count * here):
        slot = slot_ref[head]
        out_ref[:, head * DH : (head + 1) * DH] = landed[slot // here, slot % here]
    for copy in sends:
        copy.wait_send()


def finish(slot, context):
    seq_count, here, rows, _ = context.shape
    return pl.pallas_call(
        finish_kernel,
        in_specs=[pl.BlockSpec(memory_space=pltpu.SMEM), pl.BlockSpec(memory_space=pl.ANY)],
        out_specs=pl.BlockSpec(memory_space=pltpu.VMEM),
        out_shape=jax.ShapeDtypeStruct((rows, seq_count * here * DH), context.dtype),
        scratch_shapes=[
            pltpu.VMEM(context.shape, context.dtype),
            pltpu.SemaphoreType.DMA((seq_count,)),
            pltpu.SemaphoreType.DMA((seq_count,)),
            pltpu.SemaphoreType.DMA((1,)),
        ],
        compiler_params=pltpu.CompilerParams(collective_id=1, has_side_effects=True),
        name="finish",
    )(slot, context)


def attend_kernel(heads, scalar_ref, q_ref, kv_ref, doc_ref, out_ref):
    step = pl.program_id(0)
    tp = lax.axis_index("tp")
    chunks, _, _, own, _ = kv_ref.shape
    block = chunks * own
    rows = heads * own
    q = q_ref[0, :heads].reshape(rows, DH)
    place = step * block + tp * own
    first = jnp.sum((doc_ref[...] < scalar_ref[place]).astype(jnp.int32))
    docs = doc_ref[pl.ds(step * chunks + tp, 1), :]
    docs = jnp.broadcast_to(docs, (own, own)).T[:, :1]
    docs = jnp.concatenate([docs] * heads, 0)
    places = place + lax.broadcasted_iota(jnp.int32, (own, 1), 0)
    places = jnp.concatenate([places] * heads, 0)
    factor = (DH**-0.5) * LOG2_E

    def body(index, carry):
        top, total, acc = carry
        keys = kv_ref[:, index, 0].reshape(block, DH)
        values = kv_ref[:, index, 1].reshape(block, DH)
        scores = lax.dot_general(
            q, keys, (((1,), (1,)), ((), ())), preferred_element_type=jnp.float32
        )
        at = index * block + lax.broadcasted_iota(jnp.int32, (1, block), 1)
        key_docs = jnp.concatenate(
            [doc_ref[pl.ds(index * chunks + c, 1), :] for c in range(chunks)], 1
        )
        scores = jnp.where((at <= places) & (key_docs == docs), scores, NEG_BIG)
        new_top = jnp.maximum(top, jnp.max(scores, 1, keepdims=True))
        shrink = jnp.exp2((top - new_top) * factor)
        powers = jnp.exp2((scores - new_top) * factor)
        total = total * shrink + jnp.sum(powers, 1, keepdims=True)
        acc = acc * shrink + jnp.dot(
            powers.astype(jnp.bfloat16), values, preferred_element_type=jnp.float32
        )
        return new_top, total, acc

    last = place // block
    start = (
        jnp.full((rows, 1), NEG_BIG, jnp.float32),
        jnp.zeros((rows, 1), jnp.float32),
        jnp.zeros((rows, DH), jnp.float32),
    )
    carry = body(last, start)
    top, total, acc = lax.fori_loop(first // block, last, body, carry)
    out_ref[0] = (acc / total).astype(jnp.bfloat16).reshape(heads, own, DH)


def attend(document_index, q, kv, heads):
    steps, slabs, own, _ = q.shape
    return pl.pallas_call(
        functools.partial(attend_kernel, heads),
        grid_spec=pltpu.PrefetchScalarGridSpec(
            num_scalar_prefetch=1,
            grid=(steps,),
            in_specs=[
                pl.BlockSpec((1, slabs, own, DH), lambda i, *_: (i, 0, 0, 0)),
                pl.BlockSpec(kv.shape, lambda i, *_: (0,) * 5),
                pl.BlockSpec((steps * kv.shape[0], own), lambda i, *_: (0, 0)),
            ],
            out_specs=pl.BlockSpec((1, heads, own, DH), lambda i, *_: (i, 0, 0, 0)),
        ),
        out_shape=jax.ShapeDtypeStruct((steps, heads, own, DH), jnp.bfloat16),
        name="attend",
    )(document_index, q, kv, document_index.reshape(-1, own))


def head_tables(query_to_key_head):
    heads = jnp.arange(H, dtype=jnp.int32)
    same = query_to_key_head[:, None] == query_to_key_head[None, :]
    earlier = heads[None, :] < heads[:, None]
    slot = GROUP * query_to_key_head + jnp.sum((same & earlier).astype(jnp.int32), 1)
    order = jnp.sum(jnp.where(slot[None, :] == heads[:, None], heads[None, :], 0), 1)
    return order.astype(jnp.int32), slot.astype(jnp.int32)


def per_device(
    tokens,
    joined_projection_weight,
    adapter_down_weight,
    adapter_up_weight,
    document_index,
    query_to_key_head,
):
    tp_count = lax.axis_size("tp")
    seq_count = lax.axis_size("seq")
    tp_rank = lax.axis_index("tp")
    seq_rank = lax.axis_index("seq")
    own = tokens.shape[0]
    block = own * tp_count
    here = H // seq_count
    q_per, kv_per = H // tp_count, KV // tp_count

    index, slot = head_tables(query_to_key_head)
    places = (seq_rank * block + jnp.arange(block, dtype=jnp.int32)).astype(jnp.float32)
    cosine, sine = rope_tables(places)
    table = (1, tp_count // 2, 2, own, DH)
    cosine = jnp.concatenate([cosine.reshape(table), jnp.ones(table, jnp.float32)])
    sine = jnp.concatenate([sine.reshape(table), jnp.zeros(table, jnp.float32)])
    held, kv = front(
        index, tokens, joined_projection_weight, adapter_down_weight, adapter_up_weight,
        cosine, sine, tp_count, seq_count, q_per + kv_per,
    )
    context = attend(document_index, held, kv, here)
    return finish(slot, context)


def solution(mesh):
    return jax.shard_map(
        per_device,
        mesh=mesh,
        in_specs=(P(("seq", "tp"), None), P(None, "tp"), P(), P(None, "tp"), P(), P()),
        out_specs=P(("seq", "tp"), None),
        check_vma=False,
    )
```

```python
import functools

import jax
import jax.numpy as jnp
from jax import lax
from jax.experimental import pallas as pl
from jax.experimental.pallas import tpu as pltpu
from jax.sharding import PartitionSpec as P

H = 32
KV = 8
DH = 128
GROUP = H // KV

ADAPTER_SCALE = 0.5
THETA = 500000.0
NEG_BIG = -1e30
LOG2_E = 1.4426950408889634


def rope_tables(places):
    half = DH // 2
    frequency = THETA ** (-(jnp.arange(half, dtype=jnp.float32) * 2.0) / DH)
    angles = places[:, None] * frequency[None, :]
    cosine, sine = jnp.cos(angles), jnp.sin(angles)
    return jnp.concatenate([cosine, cosine], 1), jnp.concatenate([-sine, sine], 1)


MESH = pl.DeviceIdType.MESH


def front_kernel(
    rotated_pairs, here, index_ref, tokens_ref, w_ref, down_ref, up_ref, cos_ref, sin_ref,
    q_ref, kv_ref,
    x_all, w_all, stage, landed_low, landed_high, sent, mid_ref,
    w_sem, local_sem, send_sem, x_sem, land_sem, q_sem, kv_sem, spread_sem,
):
    tp = lax.axis_index("tp")
    seq = lax.axis_index("seq")
    chips, _, own, _ = x_all.shape
    halves, half = 2, own // 2
    tp_count, seq_count = 2 * chips, q_ref.shape[0]
    steps = w_all.shape[0]
    wide = w_all.shape[2]
    pair = wide // DH
    chip, core = tp // 2, tp % 2
    partner = chip * 2 + (1 - core)
    landed = (landed_low, landed_high)
    sends = []

    def send(src, dst, sem, axis, target):
        copy = pltpu.make_async_remote_copy(
            src_ref=src, dst_ref=dst, send_sem=send_sem.at[len(sends)], recv_sem=sem,
            device_id={axis: target}, device_id_type=MESH,
        )
        copy.start()
        sends.append(copy)

    def arrived(dst, sem, axis, source):
        pltpu.make_async_remote_copy(
            src_ref=dst, dst_ref=dst, send_sem=send_sem.at[0], recv_sem=sem,
            device_id={axis: source}, device_id_type=MESH,
        ).wait_recv()

    def weight_copy(step):
        return pltpu.make_async_copy(
            w_ref.at[:, pl.ds(pl.multiple_of(step * wide, wide), wide)], w_all.at[step], w_sem.at[step]
        )

    own_copy = pltpu.make_async_copy(tokens_ref, x_all.at[chip, core], local_sem.at[0])
    own_copy.start()
    for step in range(steps):
        weight_copy(step).start()

    barrier = pltpu.get_barrier_semaphore()
    for k in range(1, tp_count):
        pl.semaphore_signal(
            barrier, inc=1, device_id={"tp": (tp + k) % tp_count}, device_id_type=MESH
        )
    for k in range(1, seq_count):
        pl.semaphore_signal(
            barrier, inc=1, device_id={"seq": (seq + k) % seq_count}, device_id_type=MESH
        )
    pl.semaphore_wait(barrier, tp_count - 1 + seq_count - 1)

    def rows_of(h):
        return pl.ds(h * half, half)

    others = [(chip + k) % chips for k in range(1, chips)]
    for h in range(halves):
        for other in others:
            send(
                tokens_ref.at[rows_of(h)], x_all.at[chip, core, rows_of(h)],
                x_sem.at[chip, core, h], "tp", other * 2 + core,
            )
        send(
            tokens_ref.at[rows_of(h)], x_all.at[chip, core, rows_of(h)],
            x_sem.at[chip, core, h], "tp", partner,
        )

    def compute(where, low, count, first):
        rows = pl.ds(low, count)
        x = x_all[where, :, rows, :].reshape(2 * count, x_all.shape[3])
        mid_ref[pl.ds(0, 2 * count)] = lax.dot_general(
            x, down_ref[...], (((1,), (1,)), ((), ())), preferred_element_type=jnp.float32
        ).astype(jnp.bfloat16)

        @pl.loop(0, steps)
        def _(step):
            if first:
                weight_copy(step).wait()
            x = x_all[where, :, rows, :].reshape(2 * count, x_all.shape[3])
            joined = jnp.dot(x, w_all[step], preferred_element_type=jnp.float32)
            joined = joined + ADAPTER_SCALE * jnp.dot(
                mid_ref[pl.ds(0, 2 * count)], up_ref[:, pl.ds(pl.multiple_of(step * wide, wide), wide)],
                preferred_element_type=jnp.float32
            )
            kind = step // rotated_pairs
            cosine = cos_ref[kind, where, :, rows, :].reshape(2 * count, DH)
            sine = sin_ref[kind, where, :, rows, :].reshape(2 * count, DH)
            for head in range(pair):
                part = joined[:, head * DH : (head + 1) * DH]
                part = part * cosine + pltpu.roll(part, DH // 2, 1) * sine
                part = part.astype(jnp.bfloat16)
                for k in range(2):
                    stage[where, k, step * pair + head, rows] = part[k * count : (k + 1) * count]

    def give(where, k, h, target):
        send(
            stage.at[where, k, :, rows_of(h)], landed[h].at[tp],
            land_sem.at[tp, h], "tp", target,
        )

    own_copy.wait()
    for h in range(halves):
        arrived(x_all.at[chip, 1 - core, rows_of(h)], x_sem.at[chip, 1 - core, h], "tp", partner)
    compute(chip, 0, own, True)
    keeps = [
        pltpu.make_async_copy(
            stage.at[chip, core, :, rows_of(h)], landed[h].at[tp], local_sem.at[5 * h]
        )
        for h in range(halves)
    ]
    for keep in keeps:
        keep.start()
    for h in range(halves):
        give(chip, 1 - core, h, partner)
    for h in range(halves):
        for other in others:
            block = x_all.at[other, core, rows_of(h)]
            arrived(block, x_sem.at[other, core, h], "tp", other * 2 + core)
            send(block, block, x_sem.at[other, core, h], "tp", partner)
        for other in others:
            arrived(
                x_all.at[other, 1 - core, rows_of(h)], x_sem.at[other, 1 - core, h], "tp", partner
            )
            compute(other, h * half, half, False)
            for k in range(2):
                give(other, k, h, other * 2 + k)
    for keep in keeps:
        keep.wait()
    q_per = H // tp_count
    kv_per = KV // tp_count
    near = [(seq + k) % seq_count for k in range(1, seq_count)]
    mine = []

    def hold(src, dst):
        copy = pltpu.make_async_copy(src, dst, local_sem.at[1 + len(mine)])
        copy.start()
        mine.append(copy)

    for h in range(halves):
        rows = rows_of(h)
        for k in range(1, tp_count):
            source = (tp + k) % tp_count
            arrived(landed[h].at[source], land_sem.at[source, h], "tp", source)

        @pl.loop(0, seq_count)
        def _(j):
            kv_head = j * here // GROUP
            for k in range(2):
                sent[j, here + k, rows] = landed[h][
                    kv_head // kv_per, q_per + k * kv_per + kv_head % kv_per
                ]

        for j in near:
            send(
                sent.at[j, pl.ds(here, 2), rows], kv_ref.at[tp, seq, :, rows],
                kv_sem.at[seq, h], "seq", j,
            )

        @pl.loop(0, seq_count)
        def _(j):
            for k in range(here):
                head = index_ref[j * here + k]
                sent[j, k, rows] = landed[h][head // q_per, head % q_per]

        for j in near:
            send(
                sent.at[j, pl.ds(0, here), rows], q_ref.at[seq, :, rows],
                q_sem.at[seq, h], "seq", j,
            )
        hold(sent.at[seq, pl.ds(here, 2), rows], kv_ref.at[tp, seq, :, rows])
        hold(sent.at[seq, pl.ds(0, here), rows], q_ref.at[seq, :, rows])

    for copy in mine:
        copy.wait()
    for h in range(halves):
        for n, source in enumerate([seq] + near[::-1]):
            block = kv_ref.at[tp, source, :, rows_of(h)]
            if n:
                arrived(block, kv_sem.at[source, h], "seq", source)
            for k in range(1, tp_count):
                send(block, block, spread_sem.at[tp, source, h], "tp", (tp + k) % tp_count)
    for h in range(halves):
        for source in near:
            arrived(q_ref.at[source, :, rows_of(h)], q_sem.at[source, h], "seq", source)
        for k in range(1, tp_count):
            source = (tp + k) % tp_count
            for n in range(seq_count):
                arrived(
                    kv_ref.at[source, n, :, rows_of(h)], spread_sem.at[source, n, h], "tp", source
                )
    for copy in sends:
        copy.wait_send()


def front(index, tokens, w, down, up, cosine, sine, tp_count, seq_count, rotated_heads):
    own, width = tokens.shape
    heads = w.shape[1] // DH
    pair = 2
    steps = heads // pair
    chips = tp_count // 2
    here = H // seq_count
    rank = down.shape[1]
    vmem = pl.BlockSpec(memory_space=pltpu.VMEM)
    anywhere = pl.BlockSpec(memory_space=pl.ANY)
    count = (
        2 * chips + 2 + 2 * (chips - 1) * 4 + 4 * (seq_count - 1) + 2 * seq_count * (tp_count - 1)
    )
    bf16 = jnp.bfloat16
    return pl.pallas_call(
        functools.partial(front_kernel, rotated_heads // pair, here),
        in_specs=[pl.BlockSpec(memory_space=pltpu.SMEM), anywhere, anywhere, vmem, vmem, vmem, vmem],
        out_specs=[anywhere, anywhere],
        out_shape=[
            jax.ShapeDtypeStruct((seq_count, here, own, DH), bf16),
            jax.ShapeDtypeStruct((tp_count, seq_count, 2, own, DH), bf16),
        ],
        scratch_shapes=[
            pltpu.VMEM((chips, 2, own, width), bf16),
            pltpu.VMEM((steps, width, pair * DH), bf16),
            pltpu.VMEM((chips, 2, heads, own, DH), bf16),
            pltpu.VMEM((tp_count, heads, own // 2, DH), bf16),
            pltpu.VMEM((tp_count, heads, own // 2, DH), bf16),
            pltpu.VMEM((seq_count, here + 2, own, DH), bf16),
            pltpu.VMEM((2 * own, rank), bf16),
            pltpu.SemaphoreType.DMA((steps,)),
            pltpu.SemaphoreType.DMA((6,)),
            pltpu.SemaphoreType.DMA((count,)),
            pltpu.SemaphoreType.DMA((chips, 2, 2)),
            pltpu.SemaphoreType.DMA((tp_count, 2)),
            pltpu.SemaphoreType.DMA((seq_count, 2)),
            pltpu.SemaphoreType.DMA((seq_count, 2)),
            pltpu.SemaphoreType.DMA((tp_count, seq_count, 2)),
        ],
        compiler_params=pltpu.CompilerParams(collective_id=0, has_side_effects=True),
        name="front",
    )(index, tokens, w, down.T, up, cosine, sine)


def finish_kernel(slot_ref, in_ref, out_ref, landed, send_sem, land_sem, local_sem):
    seq = lax.axis_index("seq")
    seq_count, here, _, _ = landed.shape
    own_copy = pltpu.make_async_copy(in_ref.at[seq], landed.at[seq], local_sem.at[0])
    own_copy.start()
    near = [(seq + k) % seq_count for k in range(1, seq_count)]
    barrier = pltpu.get_barrier_semaphore()
    for j in near:
        pl.semaphore_signal(barrier, inc=1, device_id={"seq": j}, device_id_type=MESH)
    pl.semaphore_wait(barrier, seq_count - 1)
    sends = []
    for n, j in enumerate(near):
        copy = pltpu.make_async_remote_copy(
            src_ref=in_ref.at[j], dst_ref=landed.at[seq], send_sem=send_sem.at[n],
            recv_sem=land_sem.at[seq], device_id={"seq": j}, device_id_type=MESH,
        )
        copy.start()
        sends.append(copy)
    own_copy.wait()
    for j in near:
        pltpu.make_async_remote_copy(
            src_ref=landed.at[j], dst_ref=landed.at[j], send_sem=send_sem.at[0],
            recv_sem=land_sem.at[j], device_id={"seq": j}, device_id_type=MESH,
        ).wait_recv()
    for head in range(seq_count * here):
        slot = slot_ref[head]
        out_ref[:, head * DH : (head + 1) * DH] = landed[slot // here, slot % here]
    for copy in sends:
        copy.wait_send()


def finish(slot, context):
    seq_count, here, rows, _ = context.shape
    return pl.pallas_call(
        finish_kernel,
        in_specs=[pl.BlockSpec(memory_space=pltpu.SMEM), pl.BlockSpec(memory_space=pl.ANY)],
        out_specs=pl.BlockSpec(memory_space=pltpu.VMEM),
        out_shape=jax.ShapeDtypeStruct((rows, seq_count * here * DH), context.dtype),
        scratch_shapes=[
            pltpu.VMEM(context.shape, context.dtype),
            pltpu.SemaphoreType.DMA((seq_count,)),
            pltpu.SemaphoreType.DMA((seq_count,)),
            pltpu.SemaphoreType.DMA((1,)),
        ],
        compiler_params=pltpu.CompilerParams(collective_id=1, has_side_effects=True),
        name="finish",
    )(slot, context)


def attend_kernel(heads, scalar_ref, q_ref, kv_ref, doc_ref, out_ref):
    step = pl.program_id(0)
    tp = lax.axis_index("tp")
    chunks, _, _, own, _ = kv_ref.shape
    block = chunks * own
    rows = heads * own
    q = q_ref[0, :heads].reshape(rows, DH)
    place = step * block + tp * own
    first = jnp.sum((doc_ref[...] < scalar_ref[place]).astype(jnp.int32))
    docs = doc_ref[pl.ds(step * chunks + tp, 1), :]
    docs = jnp.broadcast_to(docs, (own, own)).T[:, :1]
    docs = jnp.concatenate([docs] * heads, 0)
    places = place + lax.broadcasted_iota(jnp.int32, (own, 1), 0)
    places = jnp.concatenate([places] * heads, 0)
    factor = (DH**-0.5) * LOG2_E

    def body(index, carry, own_block=False):
        top, total, acc = carry
        keys = kv_ref[:, index, 0].reshape(block, DH)
        values = kv_ref[:, index, 1].reshape(block, DH)
        scores = lax.dot_general(
            q, keys, (((1,), (1,)), ((), ())), preferred_element_type=jnp.float32
        )
        at = index * block + lax.broadcasted_iota(jnp.int32, (1, block), 1)
        key_docs = jnp.concatenate(
            [doc_ref[pl.ds(index * chunks + c, 1), :] for c in range(chunks)], 1
        )
        kept = key_docs == docs
        if own_block:
            kept = kept & (at <= places)
        scores = jnp.where(kept, scores, NEG_BIG)
        new_top = jnp.maximum(top, jnp.max(scores, 1, keepdims=True))
        shrink = jnp.exp2((top - new_top) * factor)
        powers = jnp.exp2((scores - new_top) * factor)
        total = total * shrink + jnp.sum(powers, 1, keepdims=True)
        acc = acc * shrink + jnp.dot(
            powers.astype(jnp.bfloat16), values, preferred_element_type=jnp.float32
        )
        return new_top, total, acc

    last = place // block
    start = (
        jnp.full((rows, 1), NEG_BIG, jnp.float32),
        jnp.zeros((rows, 1), jnp.float32),
        jnp.zeros((rows, DH), jnp.float32),
    )
    carry = body(last, start, True)
    top, total, acc = lax.fori_loop(first // block, last, body, carry)
    out_ref[0] = (acc / total).astype(jnp.bfloat16).reshape(heads, own, DH)


def attend(document_index, q, kv, heads):
    steps, slabs, own, _ = q.shape
    return pl.pallas_call(
        functools.partial(attend_kernel, heads),
        grid_spec=pltpu.PrefetchScalarGridSpec(
            num_scalar_prefetch=1,
            grid=(steps,),
            in_specs=[
                pl.BlockSpec((1, slabs, own, DH), lambda i, *_: (i, 0, 0, 0)),
                pl.BlockSpec(kv.shape, lambda i, *_: (0,) * 5),
                pl.BlockSpec((steps * kv.shape[0], own), lambda i, *_: (0, 0)),
            ],
            out_specs=pl.BlockSpec((1, heads, own, DH), lambda i, *_: (i, 0, 0, 0)),
        ),
        out_shape=jax.ShapeDtypeStruct((steps, heads, own, DH), jnp.bfloat16),
        name="attend",
    )(document_index, q, kv, document_index.reshape(-1, own))


def head_tables(query_to_key_head):
    heads = jnp.arange(H, dtype=jnp.int32)
    same = query_to_key_head[:, None] == query_to_key_head[None, :]
    earlier = heads[None, :] < heads[:, None]
    slot = GROUP * query_to_key_head + jnp.sum((same & earlier).astype(jnp.int32), 1)
    order = jnp.sum(jnp.where(slot[None, :] == heads[:, None], heads[None, :], 0), 1)
    return order.astype(jnp.int32), slot.astype(jnp.int32)


def per_device(
    tokens,
    joined_projection_weight,
    adapter_down_weight,
    adapter_up_weight,
    document_index,
    query_to_key_head,
):
    tp_count = lax.axis_size("tp")
    seq_count = lax.axis_size("seq")
    tp_rank = lax.axis_index("tp")
    seq_rank = lax.axis_index("seq")
    own = tokens.shape[0]
    block = own * tp_count
    here = H // seq_count
    q_per, kv_per = H // tp_count, KV // tp_count

    index, slot = head_tables(query_to_key_head)
    places = (seq_rank * block + jnp.arange(block, dtype=jnp.int32)).astype(jnp.float32)
    cosine, sine = rope_tables(places)
    table = (1, tp_count // 2, 2, own, DH)
    cosine = jnp.concatenate([cosine.reshape(table), jnp.ones(table, jnp.float32)])
    sine = jnp.concatenate([sine.reshape(table), jnp.zeros(table, jnp.float32)])
    held, kv = front(
        index, tokens, joined_projection_weight, adapter_down_weight, adapter_up_weight,
        cosine, sine, tp_count, seq_count, q_per + kv_per,
    )
    context = attend(document_index, held, kv, here)
    return finish(slot, context)


def solution(mesh):
    return jax.shard_map(
        per_device,
        mesh=mesh,
        in_specs=(P(("seq", "tp"), None), P(None, "tp"), P(), P(None, "tp"), P(), P()),
        out_specs=P(("seq", "tp"), None),
        check_vma=False,
    )
```
